32 devices in a mesh: brick: 2 (over core), chain: 16 (over z, y, x).
Axes of the slice: x: 2, y: 2, z: 4, core: 2. Of those that a mesh axis runs over, the one named last changes fastest.
Arguments:
- populations: float32 [19, 4, 512, 128], P(None, 'brick', 'chain'), may hold values from 0.5 to 1.5
- positions: float32 [2, 16, 3, 64, 256], P('brick', 'chain'), may hold values from -0.4 to 0.4
- bead_site: int32 [2, 16, 64, 256], P('brick', 'chain'), may hold values from 0 to 127
- chain_slots: int32 [2, 16, 4, 256], P('brick', 'chain'), may hold values from 0 to 2047, as said below
- send_rows: int32 [2, 16, 16, 128], P('brick', 'chain'), may hold values from 0 to 63
- send_count: int32 [2, 16, 16], P('brick', 'chain'), may hold values from 32 to 128, as said below
- migrate_list: int32 [2, 16, 2, 8], P('brick', 'chain'), may hold values from 0 to 255
- migrate_count: int32 [2, 16, 2], P('brick', 'chain'), may hold values from 0 to 8, as said below
Outputs:
- read: float32 [19, 4, 512, 128], P(None, 'brick', 'chain')
- new_positions: float32 [2, 16, 3, 64, 256], P('brick', 'chain')
- arrivals: float32 [2, 16, 2, 1536], P('brick', 'chain')
The draws below stay inside these ranges and needn't reach their ends.
Inputs may be any that keep to these rules, and one draw needn't show every extreme that they name: `send_count`: in every brick one group receives 128 live slots from every group of that brick. `chain_slots`: each entry is p * 128 + s for a group p of the same brick and a slot s below send_count[b, p, c] of this device's brick b and group c. `migrate_count`: no chain leaves for its own brick; for every group one brick receives 8 chains from every other brick.
All inputs are finite; a program needn't handle non-finite values.
Results may differ from the reference program's by a relative error of at most 0.00086.
Values may be sent and summed in bfloat16 or wider, within the bound.
No kernel may reach another device: no remote copies, remote signals or barrier semaphores. Data moves between devices by JAX's collectives and lax.ppermute only.
A program may use at most 64 MiB of HBM per device.

```python
import math
import jax
import jax.numpy as jnp
import numpy as np
from jax import lax

CX = 2
CY = 32
ROW = 128
BEADS = 64
SLOTS = 4
CH_DEV = 256
MIG_CAP = 8
BRICKS = 2
GROUPS = 16
CAP = 128
NX = 4
NY = 512


def count_parts(key):
    key_count, key_target = jax.random.split(jax.random.fold_in(key, 11))
    lowest = max(1, CAP // 4)
    counts = jax.random.randint(key_count, (BRICKS, GROUPS, GROUPS), lowest, CAP + 1)
    target = jax.random.randint(key_target, (BRICKS,), 0, GROUPS)
    full_dest = jnp.arange(GROUPS)[None, None, :] == target[:, None, None]
    return (jnp.where(full_dest, CAP, counts).astype(jnp.int32), target)


def draw_send_count(key, part):
    counts, target = count_parts(key)
    return counts


def draw_chain_slots(key, part):
    counts, target = count_parts(key)
    key_group, key_slot = jax.random.split(jax.random.fold_in(key, 23))
    sender = jax.random.randint(key_group, (BRICKS, GROUPS, SLOTS, CH_DEV), 0, GROUPS)
    random_draw = jax.random.randint(key_slot, (BRICKS, GROUPS, SLOTS, CH_DEV), 0, 1 << 20)
    brick_index = jnp.arange(BRICKS)[:, None, None, None]
    dest_index = jnp.arange(GROUPS)[None, :, None, None]
    live_limit = counts[brick_index, sender, dest_index]
    slot_index = random_draw % live_limit
    values = sender * CAP + slot_index
    at_target = dest_index == target[:, None, None, None]
    slot_axis = jnp.arange(SLOTS)[None, None, :, None]
    chain_axis = jnp.arange(CH_DEV)[None, None, None, :]
    top_place = at_target & (slot_axis == 0) & (chain_axis == 0)
    low_place = at_target & (slot_axis == 1) & (chain_axis == 0)
    values = jnp.where(top_place, GROUPS * CAP - 1, values)
    values = jnp.where(low_place, 0, values)
    return values.astype(jnp.int32)


def draw_migrate_count(key, part):
    key_count, key_target = jax.random.split(jax.random.fold_in(key, 37))
    counts = jax.random.randint(key_count, (BRICKS, GROUPS, BRICKS), 0, MIG_CAP + 1)
    target = jax.random.randint(key_target, (GROUPS,), 0, BRICKS)
    dest_index = jnp.arange(BRICKS)[None, None, :]
    source_index = jnp.arange(BRICKS)[:, None, None]
    counts = jnp.where(dest_index == target[None, :, None], MIG_CAP, counts)
    counts = jnp.where(dest_index == source_index, 0, counts)
    return counts.astype(jnp.int32)


def with_ends(entries, key, low, largest):
    longest = entries.shape.index(max(entries.shape))
    spots = []
    for shift in (0, 1):
        where = [jax.random.randint(jax.random.fold_in(key, axis), (), 0, length) for axis, length in enumerate(entries.shape)]
        where[longest] = (where[longest] + shift) % entries.shape[longest]
        spots.append(tuple(where))
    return entries.at[spots[0]].set(low).at[spots[1]].set(largest)


def block_levels(key, shape, shards, smallest, top_value):
    factor_of = 1.0
    for position, blocks in shards:
        heights = jax.random.uniform(jax.random.fold_in(jax.random.fold_in(key, 6), position), (blocks,), jnp.float32, smallest / len(shards), top_value / len(shards))
        factor_of = factor_of * jnp.repeat(jnp.exp(heights), shape[position] // blocks).reshape((-1,) + (1,) * (len(shape) - 1 - position))
    return factor_of


def setup_inputs(seed: int = 0) -> dict:
    seeds = jax.random.split(jax.random.key(seed), 9)
    return {
        "populations": jnp.clip(0.5 + 1.0 * jax.random.uniform(seeds[0], (19, NX, NY, ROW), jnp.float32) ** block_levels(seeds[0], (19, NX, NY, ROW), ((1, 2), (2, 16)), -0.2, 0.2), 0.5, 1.5),
        "positions": jnp.clip(jax.random.uniform(seeds[1], (BRICKS, GROUPS, 3, BEADS, CH_DEV), jnp.float32, -0.4, 0.4) * block_levels(seeds[1], (BRICKS, GROUPS, 3, BEADS, CH_DEV), ((0, 2), (1, 16)), -0.4, 0.0), -0.4, 0.4),
        "bead_site": with_ends(jax.random.randint(seeds[2], (BRICKS, GROUPS, BEADS, CH_DEV), 0, ROW), jax.random.fold_in(seeds[2], 1), 0, ROW - 1).astype(jnp.int32),
        "chain_slots": draw_chain_slots(jax.random.fold_in(seeds[8], 71), 0),
        "send_rows": with_ends(jax.random.randint(seeds[4], (BRICKS, GROUPS, GROUPS, CAP), 0, CX * CY), jax.random.fold_in(seeds[4], 1), 0, (CX * CY) - 1).astype(jnp.int32),
        "send_count": draw_send_count(jax.random.fold_in(seeds[8], 71), 0),
        "migrate_list": with_ends(jax.random.randint(seeds[6], (BRICKS, GROUPS, BRICKS, MIG_CAP), 0, CH_DEV), jax.random.fold_in(seeds[6], 1), 0, CH_DEV - 1).astype(jnp.int32),
        "migrate_count": draw_migrate_count(jax.random.fold_in(seeds[8], 71), 0),
    }


LATTICE_VECTORS = np.array([[0, 0, 0], [1, 0, 0], [-1, 0, 0], [0, 1, 0], [0, -1, 0], [0, 0, 1], [0, 0, -1], [1, 1, 0], [-1, -1, 0], [1, -1, 0], [-1, 1, 0], [1, 0, 1], [-1, 0, -1], [1, 0, -1], [-1, 0, 1], [0, 1, 1], [0, -1, -1], [0, 1, -1], [0, -1, 1]], np.int32)
WEIGHT_TABLE = np.array([1.0 / 3.0] + [1.0 / 18.0] * 6 + [1.0 / 36.0] * 12)
TAU_RELAX = 0.8
SPRING = 0.5
MAX_STRETCH = 4.0
highest = lax.Precision.HIGHEST

def lattice_tables():
    return (jnp.array(LATTICE_VECTORS, jnp.float32), jnp.array(WEIGHT_TABLE, jnp.float32))

def moments(populations):
    vectors, weights = lattice_tables()
    density = jnp.einsum('i,ixyz->xyz', weights, populations, precision=highest)
    momentum = jnp.einsum('ic,ixyz->cxyz', weights[:, None] * vectors, populations, precision=highest)
    return (density, momentum)

def collide(populations, density, momentum, force_field):
    vectors, weights = lattice_tables()
    velocity = (momentum + TAU_RELAX * force_field) / density
    projected = jnp.einsum('ic,cxyz->ixyz', vectors, velocity, precision=highest)
    square = lax.optimization_barrier(jnp.sum(velocity * velocity, axis=0))
    balance = density * (1.0 + 3.0 * projected + 4.5 * projected * projected - 1.5 * square)
    return populations - (populations - balance) / TAU_RELAX

def rouse_tables(bead_count):
    mode_index = jnp.arange(bead_count).astype(jnp.float32)
    mode_basis = math.sqrt(2.0 / bead_count) * jnp.cos(math.pi * mode_index[:, None] * (mode_index[None, :] + 0.5) / bead_count)
    first_row = jnp.full((1, bead_count), math.sqrt(1.0 / bead_count), jnp.float32)
    mode_basis = jnp.concatenate([first_row, mode_basis[1:]], axis=0)
    spectrum = 4.0 * jnp.sin(math.pi * mode_index / (2.0 * bead_count)) ** 2
    return (mode_basis, spectrum)

def chain_step(received, positions, sites, slots):
    row_length = received.shape[-1]
    bead_count = positions.shape[1]
    chains = positions.shape[2]
    slot_count = slots.shape[0]
    per_slot = bead_count // slot_count
    centre = sites.reshape(slot_count, per_slot, chains)[..., None]
    site_axis = jnp.arange(row_length).astype(jnp.int32)[None, None, None, :]
    kernel = 0.5 * (site_axis == centre).astype(jnp.float32)
    kernel = kernel + 0.25 * (site_axis == (centre + 1) % row_length).astype(jnp.float32)
    kernel = kernel + 0.25 * (site_axis == (centre + row_length - 1) % row_length).astype(jnp.float32)
    slot_rows = received[slots].astype(jnp.float32)
    bead_velocity = jnp.einsum('rjns,rncs->crjn', kernel, slot_rows, precision=highest).reshape(3, bead_count, chains)
    bond_vectors = positions[:, 1:, :] - positions[:, :-1, :]
    stretch = lax.optimization_barrier(jnp.sum(bond_vectors * bond_vectors, axis=(0, 1))) / (bead_count - 1)
    stiffness = SPRING / (1.0 - stretch / MAX_STRETCH)
    mode_basis, spectrum = rouse_tables(bead_count)
    mode_amps = jnp.einsum('pj,cjn->cpn', mode_basis, positions + bead_velocity, precision=highest)
    mode_amps = mode_amps / (1.0 + stiffness[None, None, :] * spectrum[None, :, None])
    moved_beads = jnp.einsum('pj,cpn->cjn', mode_basis, mode_amps, precision=highest)
    bead_force = bead_velocity - (moved_beads - positions)
    spread = -jnp.einsum('rjns,crjn->rncs', kernel, bead_force.reshape(3, slot_count, per_slot, chains), precision=highest)
    slot_force = jnp.zeros((received.shape[0], 3, row_length), jnp.float32).at[slots.reshape(-1)].add(spread.reshape(-1, 3, row_length))
    return (moved_beads, slot_force.astype(jnp.bfloat16))

def pack_moves(moved_beads, targets, counts):
    bricks, slots_out = targets.shape
    chosen = moved_beads[:, :, targets.reshape(-1)].reshape(3, moved_beads.shape[1], bricks, slots_out).transpose(2, 3, 0, 1)
    kept_slot = jnp.arange(slots_out)[None, :] < counts[:, None]
    return jnp.where(kept_slot[:, :, None, None], chosen, jnp.zeros((), jnp.float32)).reshape(bricks, -1)

def owner_rows(values, rows):
    return jnp.zeros((CX * CY, 3, ROW), jnp.float32).at[rows.reshape(-1)].add(values.reshape(-1, 3, ROW))

def reference(populations, positions, bead_site, chain_slots, send_rows, send_count, migrate_list, migrate_count):
    density, momentum = moments(populations)
    velocity = momentum / density
    row_field = velocity.reshape(3, BRICKS, CX, GROUPS, CY, ROW).transpose(1, 3, 2, 4, 0, 5).reshape(BRICKS, GROUPS, CX * CY, 3, ROW).astype(jnp.bfloat16)
    live_slot = jnp.arange(CAP)[None, None, None, :] < send_count[..., None]
    brick_ids = jnp.arange(BRICKS)[:, None, None, None]
    sender_ids = jnp.arange(GROUPS)[None, :, None, None]
    sent = row_field[brick_ids, sender_ids, send_rows]
    sent = jnp.where(live_slot[..., None, None], sent, jnp.zeros((), jnp.bfloat16))
    received = sent.transpose(0, 2, 1, 3, 4, 5).reshape(BRICKS * GROUPS, GROUPS * CAP, 3, ROW)

    def one_device(items):
        return chain_step(items[0], items[1], items[2], items[3])
    moved_beads, slot_force = lax.map(one_device, (received, positions.reshape(BRICKS * GROUPS, 3, BEADS, CH_DEV), bead_site.reshape(BRICKS * GROUPS, BEADS, CH_DEV), chain_slots.reshape(BRICKS * GROUPS, SLOTS, CH_DEV)))
    returned = slot_force.reshape(BRICKS, GROUPS, GROUPS, CAP, 3, ROW).transpose(0, 2, 1, 3, 4, 5).astype(jnp.float32)
    returned = jnp.where(live_slot[..., None, None], returned, jnp.zeros((), jnp.float32))
    force_rows = jax.vmap(owner_rows)(returned.reshape(BRICKS * GROUPS, GROUPS * CAP, 3, ROW), send_rows.reshape(BRICKS * GROUPS, GROUPS * CAP))
    force_field = force_rows.reshape(BRICKS, GROUPS, CX, CY, 3, ROW).transpose(4, 0, 2, 1, 3, 5).reshape(3, NX, NY, ROW)
    collided = collide(populations, density, momentum, force_field)
    outputs = []
    for direction in range(19):
        shift_x, shift_y, shift_z = [int(value) for value in LATTICE_VECTORS[direction]]
        outputs.append(jnp.roll(collided[direction], (shift_x, shift_y, shift_z), axis=(0, 1, 2)))
    read = jnp.stack(outputs)
    packed = jax.vmap(pack_moves)(moved_beads, migrate_list.reshape(BRICKS * GROUPS, BRICKS, MIG_CAP), migrate_count.reshape(BRICKS * GROUPS, BRICKS))
    arrivals = packed.reshape(BRICKS, GROUPS, BRICKS, MIG_CAP * 3 * BEADS).transpose(2, 1, 0, 3)
    return (read, moved_beads.reshape(BRICKS, GROUPS, 3, BEADS, CH_DEV), arrivals)
```

```python
import functools
import math

import jax
import jax.numpy as jnp
import numpy as np
from jax import lax
from jax.experimental import pallas as pl
from jax.experimental.pallas import tpu as pltpu
from jax.sharding import PartitionSpec as P

LATTICE_VECTORS = np.array(
    [
        [0, 0, 0],
        [1, 0, 0],
        [-1, 0, 0],
        [0, 1, 0],
        [0, -1, 0],
        [0, 0, 1],
        [0, 0, -1],
        [1, 1, 0],
        [-1, -1, 0],
        [1, -1, 0],
        [-1, 1, 0],
        [1, 0, 1],
        [-1, 0, -1],
        [1, 0, -1],
        [-1, 0, 1],
        [0, 1, 1],
        [0, -1, -1],
        [0, 1, -1],
        [0, -1, 1],
    ],
    np.int32,
)
WEIGHT_TABLE = [1.0 / 3.0] + [1.0 / 18.0] * 6 + [1.0 / 36.0] * 12
DIRECTIONS = len(WEIGHT_TABLE)
VECTORS = [tuple(int(v) for v in row) for row in LATTICE_VECTORS]
MOVES_UP = [i for i in range(DIRECTIONS) if VECTORS[i][1] == 1]
MOVES_DOWN = [i for i in range(DIRECTIONS) if VECTORS[i][1] == -1]
CROSSING = [i for i in range(DIRECTIONS) if VECTORS[i][0] != 0]
TAU_RELAX = 0.8
SPRING = 0.5
MAX_STRETCH = 4.0
f32 = jnp.float32
bf16 = jnp.bfloat16
highest = lax.Precision.HIGHEST
NT = (((1,), (1,)), ((), ()))
VMEM = pl.BlockSpec(memory_space=pltpu.VMEM)
SMEM = pl.BlockSpec(memory_space=pltpu.SMEM)
ANY = pl.BlockSpec(memory_space=pl.ANY)


class Plan:
    def __init__(self, groups, rows, size_y):
        self.groups = groups
        self.outer = 4
        self.inner = groups // self.outer
        self.rows = rows
        self.size_y = size_y
        self.size_x = rows // size_y
        extra = max(self.inner, 2 * self.size_x)
        self.stride = (rows + extra + 7) // 8 * 8
        self.block = self.outer * self.stride

    def outer_shift(self, k):
        z_count, w_count = self.outer, self.inner
        return [
            (z * w_count + w, (z + k) % z_count * w_count + w)
            for z in range(z_count)
            for w in range(w_count)
        ]

    def inner_swap(self, m):
        z_count, w_count = self.outer, self.inner
        return [
            (z * w_count + w, z * w_count + (w ^ m))
            for z in range(z_count)
            for w in range(w_count)
        ]


def rouse_tables(bead_count):
    mode = np.arange(bead_count, dtype=np.float64)
    basis = math.sqrt(2.0 / bead_count) * np.cos(
        math.pi * mode[:, None] * (mode[None, :] + 0.5) / bead_count
    )
    basis[0] = math.sqrt(1.0 / bead_count)
    spectrum = 4.0 * np.sin(math.pi * mode / (2.0 * bead_count)) ** 2
    return (basis.astype(np.float32), spectrum.astype(np.float32)[:, None])


def weighted_sums(get):
    density = None
    momentum = [None, None, None]
    for i in range(DIRECTIONS):
        value = get(i) * np.float32(WEIGHT_TABLE[i])
        density = value if density is None else density + value
        for k in range(3):
            sign = VECTORS[i][k]
            if sign == 0:
                continue
            term = value if sign > 0 else -value
            momentum[k] = term if momentum[k] is None else momentum[k] + term
    return (density, momentum)


def moment_kernel(plan, pop_ref, rows_ref, count_ref, *outs):
    msg_refs = outs[: plan.outer]
    up_ref, down_ref = outs[plan.outer :]
    length = pop_ref.shape[3]
    size_y = plan.size_y
    for x in range(plan.size_x):
        density, momentum = weighted_sums(lambda i: pop_ref[i, x])
        first = slice(x * size_y, (x + 1) * size_y)
        for k in range(3):
            velocity = (momentum[k] / density).astype(bf16)
            for msg in msg_refs:
                msg[first, k * length : (k + 1) * length] = velocity
        for out, moves, row in ((up_ref, MOVES_UP, size_y - 1), (down_ref, MOVES_DOWN, 0)):
            for slot, i in enumerate(moves):
                out[slot, x : x + 1, :] = pop_ref[i, x, row : row + 1, :]
            at = len(moves)
            for slot, value in enumerate([density] + momentum):
                out[at + slot, x : x + 1, :] = value[row : row + 1]
    me = lax.axis_index("chain")
    z = me // plan.inner
    w = me % plan.inner
    lane = lax.broadcasted_iota(jnp.int32, (1, length), 1)
    extra = plan.stride - plan.rows
    for k, msg in enumerate(msg_refs):
        tables = []
        for m in range(plan.inner):
            target = (z + plan.outer - k) % plan.outer * plan.inner + (w ^ m)
            row = rows_ref[pl.ds(target, 1), :]
            tables.append(jnp.where(lane < count_ref[target], row, -1).astype(f32))
        if extra > plan.inner:
            tables.append(jnp.zeros((extra - plan.inner, length), f32))
        block = jnp.concatenate(tables, axis=0).astype(bf16)
        msg[plan.rows :, :length] = block
        msg[plan.rows :, length:] = jnp.zeros((extra, 2 * length), bf16)


def chain_kernel(plan, capacity, *refs):
    block_refs = refs[: plan.inner]
    (
        pos_ref,
        site_ref,
        slot_ref,
        list_ref,
        live_ref,
        basis_ref,
        spectrum_ref,
        own_ref,
    ) = refs[plan.inner : plan.inner + 8]
    send_refs = refs[plan.inner + 8 : 2 * plan.inner + 7]
    (
        moved_ref,
        stay_ref,
        leave_ref,
        table,
        turned,
        onehot,
        smooth,
        velocity,
        force,
        spread_hi,
        spread_lo,
        sums,
    ) = refs[2 * plan.inner + 7 :]
    inner, outer, rows, stride = plan.inner, plan.outer, plan.rows, plan.stride
    groups = plan.groups
    total = inner * plan.block
    length = table.shape[1] // 3
    slots, chains = slot_ref.shape
    beads = pos_ref.shape[1]
    per_slot = beads // slots
    extra = stride - rows
    me = lax.axis_index("chain")
    z = me // inner
    w = me % inner

    table_rows = []
    for m in range(inner):
        for k in range(outer):
            base = k * stride
            to = (m * outer + k) * stride
            table[to : to + rows, :] = block_refs[m][base : base + rows, :]
            table[to + rows : to + stride, :] = jnp.zeros((extra, 3 * length), bf16)
            names = block_refs[m][base + rows : base + stride, :length].astype(f32)
            table_rows.append(names[m : m + 1])
    names = jnp.concatenate(table_rows, axis=0).astype(bf16)

    eye = (
        lax.broadcasted_iota(jnp.int32, (length, length), 0)
        == lax.broadcasted_iota(jnp.int32, (length, length), 1)
    )
    eye = jnp.where(eye, 1.0, 0.0).astype(bf16)
    for k in range(3):
        part = slice(k * length, (k + 1) * length)
        turned[part, :] = lax.dot_general(
            eye, table[:, part], NT, preferred_element_type=f32
        ).astype(bf16)

    site_iota = lax.broadcasted_iota(jnp.int32, (length, chains), 0)
    group_iota = lax.broadcasted_iota(jnp.int32, (groups, chains), 0)
    row_iota = lax.broadcasted_iota(jnp.int32, (rows, chains), 0)
    extra_iota = lax.broadcasted_iota(jnp.int32, (extra, chains), 0)

    def group_of(p):
        return ((p % inner) ^ w) * outer + (p // inner - z + outer) % outer

    for r in range(slots):
        slot = slot_ref[r : r + 1, :]
        p = slot // capacity
        s = slot % capacity
        group = group_of(p)
        pick = jnp.where(site_iota == s, 1.0, 0.0).astype(bf16)
        looked = jnp.dot(names, pick, preferred_element_type=f32)
        row = jnp.sum(jnp.where(group_iota == group, looked, 0.0), axis=0, keepdims=True)
        row = row.astype(jnp.int32)
        live = row >= 0
        y = row % plan.size_y
        x = row // plan.size_y
        first = jnp.where(live, group * stride + row, -1)
        above = group_of((p + 1) % groups) * stride + x
        below = group_of((p + groups - 1) % groups) * stride + plan.size_x + x
        second = jnp.where(y == plan.size_y - 1, above, jnp.where(y == 0, below, -stride))
        second = jnp.where(live, second, -stride)
        lanes = slice(r * chains, (r + 1) * chains)
        for g in range(groups):
            base = g * stride
            onehot[base : base + rows, lanes] = jnp.where(
                row_iota == first - base, 1.0, 0.0
            ).astype(bf16)
            onehot[base + rows : base + stride, lanes] = jnp.where(
                extra_iota == second - base, 1.0, 0.0
            ).astype(bf16)

    picked = jnp.dot(turned[...], onehot[...], preferred_element_type=f32).astype(bf16)
    near = lax.broadcasted_iota(jnp.int32, (length, length), 0)
    near = near - lax.broadcasted_iota(jnp.int32, (length, length), 1)
    around = (near == 1) | (near == -1) | (near == length - 1) | (near == 1 - length)
    kernel = jnp.where(near == 0, 0.5, jnp.where(around, 0.25, 0.0)).astype(bf16)
    for k in range(3):
        part = slice(k * length, (k + 1) * length)
        smooth[part, :] = jnp.dot(kernel, picked[part], preferred_element_type=f32)

    for r in range(slots):
        for octet in range(per_slot // 8):
            for tile in range(chains // 128):
                at = slice(r * per_slot + octet * 8, r * per_slot + octet * 8 + 8)
                lanes = slice(tile * 128, tile * 128 + 128)
                wide = slice(r * chains + tile * 128, r * chains + tile * 128 + 128)
                site = site_ref[at, lanes]
                inside = site & 7
                which = site >> 3
                for k in range(3):
                    value = jnp.zeros((8, 128), f32)
                    for t in range(length // 8):
                        rows8 = slice(k * length + t * 8, k * length + t * 8 + 8)
                        got = jnp.take_along_axis(
                            smooth[rows8, wide], inside, axis=0, mode="promise_in_bounds"
                        )
                        value = jnp.where(which == t, got, value)
                    velocity[k, at, lanes] = value

    stretch = None
    for k in range(3):
        bond = pos_ref[k, 1:, :] - pos_ref[k, : beads - 1, :]
        part = jnp.sum(bond * bond, axis=0, keepdims=True)
        stretch = part if stretch is None else stretch + part
    stretch = stretch / (beads - 1)
    stiffness = SPRING / (1.0 - stretch / MAX_STRETCH)
    damping = 1.0 / (1.0 + spectrum_ref[...] * stiffness)
    basis = basis_ref[...]
    for k in range(3):
        amps = jnp.dot(
            basis, pos_ref[k] + velocity[k], precision=highest, preferred_element_type=f32
        )
        moved = lax.dot_general(
            basis,
            amps * damping,
            (((0,), (0,)), ((), ())),
            precision=highest,
            preferred_element_type=f32,
        )
        moved_ref[k] = moved
        force[k] = (moved - pos_ref[k]) - velocity[k]

    brick = lax.axis_index("brick")
    chain_iota = lax.broadcasted_iota(jnp.int32, (1, chains), 1)
    leaving = list_ref.shape[1]
    for i, out in enumerate((stay_ref, leave_ref)):
        target = brick ^ i
        chosen = []
        for s in range(leaving):
            number = jnp.where(s < live_ref[target], list_ref[target, s], -1)
            chosen.append(jnp.where(chain_iota == number, 1.0, 0.0))
        chosen = jnp.concatenate(chosen, axis=0)
        for k in range(3):
            out[:, k * beads : (k + 1) * beads] = lax.dot_general(
                chosen, moved_ref[k], NT, precision=highest, preferred_element_type=f32
            )

    step = 32
    step_iota = lax.broadcasted_iota(jnp.int32, (step, 128), 0)
    for r in range(slots):
        for tile in range(chains // 128):
            lanes = slice(tile * 128, tile * 128 + 128)
            wide = slice(r * chains + tile * 128, r * chains + tile * 128 + 128)
            for start in range(0, length, step):
                parts = [jnp.zeros((step, 128), f32) for _ in range(3)]
                for j in range(per_slot):
                    at = slice(r * per_slot + j, r * per_slot + j + 1)
                    here = step_iota == site_ref[at, lanes] - start
                    for k in range(3):
                        parts[k] = parts[k] + jnp.where(here, force[k, at, lanes], 0.0)
                for k in range(3):
                    out = slice(k * length + start, k * length + start + step)
                    hi = parts[k].astype(bf16)
                    spread_hi[out, wide] = hi
                    spread_lo[out, wide] = (parts[k] - hi.astype(f32)).astype(bf16)

    sums[...] = lax.dot_general(
        onehot[...], spread_hi[...], NT, preferred_element_type=f32
    ) + lax.dot_general(onehot[...], spread_lo[...], NT, preferred_element_type=f32)
    own_ref[...] = sums[: plan.block, :]
    for m in range(1, inner):
        send_refs[m - 1][...] = sums[m * plan.block : (m + 1) * plan.block, :].astype(bf16)


def equilibrium(i, density, velocity, square):
    projected = None
    for k in range(3):
        sign = VECTORS[i][k]
        if sign == 0:
            continue
        term = velocity[k] if sign > 0 else -velocity[k]
        projected = term if projected is None else projected + term
    if projected is None:
        return density * (1.0 - 1.5 * square)
    return density * (1.0 + 3.0 * projected + 4.5 * projected * projected - 1.5 * square)


def collide_kernel(plan, pop_ref, *refs):
    kept_ref = refs[0]
    came_refs = refs[1 : plan.outer]
    low_ref, high_ref, read_ref, send_ref = refs[plan.outer :]
    length = pop_ref.shape[3]
    size_x, size_y, rows = plan.size_x, plan.size_y, plan.rows
    total = kept_ref[...]
    for came in came_refs:
        total = total + came[...].astype(f32)
    force = []
    for k in range(3):
        value = total[:, k * length : (k + 1) * length]
        near = pltpu.roll(value, 1, axis=1) + pltpu.roll(value, length - 1, axis=1)
        force.append(0.5 * value + 0.25 * near)

    def flow(density, momentum, field):
        velocity = [(momentum[k] + TAU_RELAX * field[k]) / density for k in range(3)]
        square = velocity[0] * velocity[0] + velocity[1] * velocity[1] + velocity[2] * velocity[2]
        return (density, velocity, square)

    def relax(i, value, state):
        return value - (value - equilibrium(i, *state)) / TAU_RELAX

    edges = {}
    for side, (ref, moves) in enumerate(((low_ref, MOVES_UP), (high_ref, MOVES_DOWN))):
        at = len(moves)
        first = rows + side * size_x
        state = flow(
            ref[at],
            [ref[at + 1], ref[at + 2], ref[at + 3]],
            [force[k][first : first + size_x] for k in range(3)],
        )
        for slot, i in enumerate(moves):
            edges[i] = relax(i, ref[slot], state)

    y_iota = lax.broadcasted_iota(jnp.int32, (size_y, length), 0)
    for x in range(size_x):
        density, momentum = weighted_sums(lambda i: pop_ref[i, x])
        state = flow(
            density, momentum, [force[k][x * size_y : (x + 1) * size_y] for k in range(3)]
        )
        for i in range(DIRECTIONS):
            shift_x, shift_y, shift_z = VECTORS[i]
            value = relax(i, pop_ref[i, x], state)
            if shift_y != 0:
                value = pltpu.roll(value, shift_y % size_y, axis=0)
                edge = jnp.broadcast_to(edges[i][x : x + 1], (size_y, length))
                value = jnp.where(y_iota == (0 if shift_y > 0 else size_y - 1), edge, value)
            if shift_z != 0:
                value = pltpu.roll(value, shift_z % length, axis=1)
            target = x + shift_x
            if 0 <= target < size_x:
                read_ref[i, target] = value
            else:
                send_ref[CROSSING.index(i)] = value


def merge_kernel(plan, came_ref, part_ref, read_ref, sem):
    del part_ref
    copies = []
    for slot, i in enumerate(CROSSING):
        target = 0 if VECTORS[i][0] > 0 else plan.size_x - 1
        copies.append(
            pltpu.make_async_copy(came_ref.at[slot], read_ref.at[i, target], sem.at[slot])
        )
    for copy in copies:
        copy.start()
    for copy in copies:
        copy.wait()


def local(
    populations,
    positions,
    bead_site,
    chain_slots,
    send_rows,
    send_count,
    migrate_list,
    migrate_count,
):
    size_x, size_y, length = populations.shape[1:]
    groups = lax.axis_size("chain")
    bricks = lax.axis_size("brick")
    capacity = send_rows.shape[-1]
    plan = Plan(groups, size_x * size_y, size_y)
    inner, outer = plan.inner, plan.outer
    beads, chains = positions.shape[3:]
    slots = chain_slots.shape[2]
    shape = jax.ShapeDtypeStruct
    width = 3 * length
    edge = shape((len(MOVES_UP) + 4, size_x, length), f32)

    first = pl.pallas_call(
        functools.partial(moment_kernel, plan),
        out_shape=[shape((plan.stride, width), bf16)] * outer + [edge, edge],
        in_specs=[VMEM, VMEM, SMEM],
        out_specs=[VMEM] * (outer + 2),
        name="moments",
    )(populations, send_rows[0, 0], send_count[0, 0])
    msgs, (edge_up, edge_down) = first[:outer], first[outer:]
    parts = [msgs[0]] + [
        lax.ppermute(msgs[k], "chain", plan.outer_shift(-k)) for k in range(1, outer)
    ]
    near = jnp.concatenate(parts, axis=0)
    blocks = [near] + [lax.ppermute(near, "chain", plan.inner_swap(m)) for m in range(1, inner)]
    up = [(i, (i + 1) % groups) for i in range(groups)]
    down = [(j, i) for i, j in up]
    low = lax.ppermute(edge_up, "chain", up)
    high = lax.ppermute(edge_down, "chain", down)

    basis, spectrum = rouse_tables(beads)
    total = inner * plan.block
    leaving = migrate_list.shape[-1]
    second = pl.pallas_call(
        functools.partial(chain_kernel, plan, capacity),
        out_shape=[shape((plan.block, width), f32)]
        + [shape((plan.block, width), bf16)] * (inner - 1)
        + [shape((3, beads, chains), f32)]
        + [shape((leaving, 3 * beads), f32)] * 2,
        in_specs=[VMEM] * (inner + 3) + [SMEM, SMEM] + [VMEM, VMEM],
        out_specs=[VMEM] * (inner + 3),
        scratch_shapes=[
            pltpu.VMEM((total, width), bf16),
            pltpu.VMEM((width, total), bf16),
            pltpu.VMEM((total, slots * chains), bf16),
            pltpu.VMEM((width, slots * chains), f32),
            pltpu.VMEM((3, beads, chains), f32),
            pltpu.VMEM((3, beads, chains), f32),
            pltpu.VMEM((width, slots * chains), bf16),
            pltpu.VMEM((width, slots * chains), bf16),
            pltpu.VMEM((total, width), f32),
        ],
        name="chains",
    )(
        *blocks,
        positions[0, 0],
        bead_site[0, 0],
        chain_slots[0, 0],
        migrate_list[0, 0],
        migrate_count[0, 0],
        basis,
        spectrum,
    )
    own, sends = second[0], second[1:inner]
    moved, stay, leave = second[inner:]
    total_force = own
    for m in range(1, inner):
        total_force = total_force + lax.ppermute(sends[m - 1], "chain", plan.inner_swap(m)).astype(
            f32
        )
    swap = [(i, (i + 1) % bricks) for i in range(bricks)]
    arrived = lax.ppermute(leave, "brick", swap)
    stride = plan.stride
    kept = total_force[:stride]
    came = [
        lax.ppermute(
            total_force[k * stride : (k + 1) * stride].astype(bf16), "chain", plan.outer_shift(k)
        )
        for k in range(1, outer)
    ]
    partial, crossing = pl.pallas_call(
        functools.partial(collide_kernel, plan),
        out_shape=[
            shape(populations.shape, f32),
            shape((len(CROSSING), size_y, length), f32),
        ],
        in_specs=[VMEM] * (outer + 3),
        out_specs=[VMEM, VMEM],
        name="collide",
    )(populations, kept, *came, low, high)
    crossed = lax.ppermute(crossing, "brick", swap)
    read = pl.pallas_call(
        functools.partial(merge_kernel, plan),
        out_shape=shape(populations.shape, f32),
        in_specs=[VMEM, ANY],
        out_specs=ANY,
        scratch_shapes=[pltpu.SemaphoreType.DMA((len(CROSSING),))],
        input_output_aliases={1: 0},
        name="merge",
    )(crossed, partial)
    here = lax.axis_index("brick")
    stay = stay.reshape(1, -1)
    arrived = arrived.reshape(1, -1)
    arrivals = jnp.where(
        here == 0,
        jnp.concatenate([stay, arrived], axis=0),
        jnp.concatenate([arrived, stay], axis=0),
    )
    return (read, moved[None, None], arrivals[None, None])


def solution(mesh):
    placed = (
        P(None, "brick", "chain", None),
        P("brick", "chain", None, None, None),
        P("brick", "chain", None, None),
        P("brick", "chain", None, None),
        P("brick", "chain", None, None),
        P("brick", "chain", None),
        P("brick", "chain", None, None),
        P("brick", "chain", None),
    )
    return jax.shard_map(
        local,
        mesh=mesh,
        in_specs=placed,
        out_specs=(
            P(None, "brick", "chain", None),
            P("brick", "chain", None, None, None),
            P("brick", "chain", None, None),
        ),
        check_vma=False,
    )
```

```python
import functools
import math

import jax
import jax.numpy as jnp
import numpy as np
from jax import lax
from jax.experimental import pallas as pl
from jax.experimental.pallas import tpu as pltpu
from jax.sharding import PartitionSpec as P

LATTICE_VECTORS = np.array(
    [
        [0, 0, 0],
        [1, 0, 0],
        [-1, 0, 0],
        [0, 1, 0],
        [0, -1, 0],
        [0, 0, 1],
        [0, 0, -1],
        [1, 1, 0],
        [-1, -1, 0],
        [1, -1, 0],
        [-1, 1, 0],
        [1, 0, 1],
        [-1, 0, -1],
        [1, 0, -1],
        [-1, 0, 1],
        [0, 1, 1],
        [0, -1, -1],
        [0, 1, -1],
        [0, -1, 1],
    ],
    np.int32,
)
WEIGHT_TABLE = [1.0 / 3.0] + [1.0 / 18.0] * 6 + [1.0 / 36.0] * 12
DIRECTIONS = len(WEIGHT_TABLE)
VECTORS = [tuple(int(v) for v in row) for row in LATTICE_VECTORS]
MOVES_UP = [i for i in range(DIRECTIONS) if VECTORS[i][1] == 1]
MOVES_DOWN = [i for i in range(DIRECTIONS) if VECTORS[i][1] == -1]
CROSSING = [i for i in range(DIRECTIONS) if VECTORS[i][0] != 0]
TAU_RELAX = 0.8
SPRING = 0.5
MAX_STRETCH = 4.0
f32 = jnp.float32
bf16 = jnp.bfloat16
highest = lax.Precision.HIGHEST
NT = (((1,), (1,)), ((), ()))
VMEM = pl.BlockSpec(memory_space=pltpu.VMEM)
SMEM = pl.BlockSpec(memory_space=pltpu.SMEM)
ANY = pl.BlockSpec(memory_space=pl.ANY)
HBM = pl.BlockSpec(memory_space=pltpu.HBM)


class Plan:
    def __init__(self, groups, rows, size_y):
        self.groups = groups
        self.outer = 4
        self.inner = groups // self.outer
        self.rows = rows
        self.size_y = size_y
        self.size_x = rows // size_y
        self.extra = max(self.inner, 2 * self.size_x)
        self.stride = (rows + self.extra + 7) // 8 * 8
        self.main = self.outer * rows
        self.block = (self.main + self.outer * self.extra + 15) // 16 * 16

    def outer_shift(self, k):
        z_count, w_count = self.outer, self.inner
        return [
            (z * w_count + w, (z + k) % z_count * w_count + w)
            for z in range(z_count)
            for w in range(w_count)
        ]

    def inner_swap(self, m):
        z_count, w_count = self.outer, self.inner
        return [
            (z * w_count + w, z * w_count + (w ^ m))
            for z in range(z_count)
            for w in range(w_count)
        ]


def rouse_tables(bead_count):
    mode = np.arange(bead_count, dtype=np.float64)
    basis = math.sqrt(2.0 / bead_count) * np.cos(
        math.pi * mode[:, None] * (mode[None, :] + 0.5) / bead_count
    )
    basis[0] = math.sqrt(1.0 / bead_count)
    spectrum = 4.0 * np.sin(math.pi * mode / (2.0 * bead_count)) ** 2
    return (basis.astype(np.float32), spectrum.astype(np.float32)[:, None])


def weighted_sums(get):
    density = None
    momentum = [None, None, None]
    for i in range(DIRECTIONS):
        value = get(i) * np.float32(WEIGHT_TABLE[i])
        density = value if density is None else density + value
        for k in range(3):
            sign = VECTORS[i][k]
            if sign == 0:
                continue
            term = value if sign > 0 else -value
            momentum[k] = term if momentum[k] is None else momentum[k] + term
    return (density, momentum)


def moment_kernel(plan, pop_hbm, rows_hbm, count_hbm, slots_hbm, *outs):
    msg_refs = outs[: plan.outer]
    up_ref, down_ref, state_ref, slots_ref, pop_ref, rows_ref, count_ref, sem = outs[
        plan.outer :
    ]
    length = pop_ref.shape[3]
    size_x, size_y = plan.size_x, plan.size_y
    loads = [
        pltpu.make_async_copy(pop_hbm.at[:, x], pop_ref.at[:, x], sem.at[x])
        for x in range(size_x)
    ]
    others = [
        pltpu.make_async_copy(rows_hbm, rows_ref, sem.at[size_x]),
        pltpu.make_async_copy(count_hbm, count_ref, sem.at[size_x + 1]),
        pltpu.make_async_copy(slots_hbm, slots_ref, sem.at[size_x + 2]),
    ]
    for copy in loads + others:
        copy.start()
    for x in range(size_x):
        loads[x].wait()
        density, momentum = weighted_sums(lambda i: pop_ref[i, x])
        first = slice(x * size_y, (x + 1) * size_y)
        for slot, value in enumerate([density] + momentum):
            state_ref[slot, first, :] = value
        for k in range(3):
            velocity = (momentum[k] / density).astype(bf16)
            for msg in msg_refs:
                msg[first, k * length : (k + 1) * length] = velocity
        for out, moves, row in ((up_ref, MOVES_UP, size_y - 1), (down_ref, MOVES_DOWN, 0)):
            for slot, i in enumerate(moves):
                out[slot, x : x + 1, :] = pop_ref[i, x, row : row + 1, :]
            at = len(moves)
            for slot, value in enumerate([density] + momentum):
                out[at + slot, x : x + 1, :] = value[row : row + 1]
    for copy in others:
        copy.wait()
    me = lax.axis_index("chain")
    z = me // plan.inner
    w = me % plan.inner
    lane = lax.broadcasted_iota(jnp.int32, (1, length), 1)
    extra = plan.stride - plan.rows
    for k, msg in enumerate(msg_refs):
        tables = []
        for m in range(plan.inner):
            target = (z + plan.outer - k) % plan.outer * plan.inner + (w ^ m)
            row = rows_ref[pl.ds(target, 1), :]
            tables.append(jnp.where(lane < count_ref[target], row, -1).astype(f32))
        if extra > plan.inner:
            tables.append(jnp.zeros((extra - plan.inner, length), f32))
        block = jnp.concatenate(tables, axis=0).astype(bf16)
        msg[plan.rows :, :length] = block
        msg[plan.rows :, length:] = jnp.zeros((extra, 2 * length), bf16)


def pack_kernel(plan, *refs):
    part_refs, out_ref = refs[:-1], refs[-1]
    rows, extra = plan.rows, plan.extra
    tails = []
    for k, part in enumerate(part_refs):
        out_ref[k * rows : (k + 1) * rows, :] = part[:rows, :]
        tails.append(part[rows:, :].astype(f32)[:extra])
    spare = plan.block - plan.main - plan.outer * extra
    if spare:
        tails.append(jnp.zeros((spare, out_ref.shape[1]), f32))
    out_ref[plan.main :, :] = jnp.concatenate(tails, axis=0).astype(bf16)


def chain_kernel(plan, capacity, *refs):
    block_refs = refs[: plan.inner]
    (
        pos_ref,
        site_ref,
        slot_ref,
        list_hbm,
        live_hbm,
        basis_ref,
        spectrum_ref,
        own_ref,
    ) = refs[plan.inner : plan.inner + 8]
    send_refs = refs[plan.inner + 8 : 2 * plan.inner + 7]
    (
        moved_ref,
        stay_ref,
        leave_ref,
        table,
        turned,
        onehot,
        smooth,
        velocity,
        force,
        spread,
        sums,
        list_ref,
        live_ref,
        sem,
    ) = refs[2 * plan.inner + 7 :]
    inner, outer, rows, extra = plan.inner, plan.outer, plan.rows, plan.extra
    main, block, groups = plan.main, plan.block, plan.groups
    length = table.shape[1] // 3
    slots, chains = slot_ref.shape
    beads = pos_ref.shape[1]
    per_slot = beads // slots
    me = lax.axis_index("chain")
    z = me // inner
    w = me % inner

    loads = [
        pltpu.make_async_copy(list_hbm, list_ref, sem.at[0]),
        pltpu.make_async_copy(live_hbm, live_ref, sem.at[1]),
    ]
    for copy in loads:
        copy.start()

    table_rows = []
    for m in range(inner):
        table[m * block : m * block + main, :] = block_refs[m][:main, :]
        table[m * block + main : (m + 1) * block, :] = jnp.zeros(
            (block - main, 3 * length), bf16
        )
        names = block_refs[m][main:, :length].astype(f32)
        for k in range(outer):
            table_rows.append(names[k * extra + m : k * extra + m + 1])
    names = jnp.concatenate(table_rows, axis=0).astype(bf16)

    eye = (
        lax.broadcasted_iota(jnp.int32, (length, length), 0)
        == lax.broadcasted_iota(jnp.int32, (length, length), 1)
    )
    eye = jnp.where(eye, 1.0, 0.0).astype(bf16)
    for k in range(3):
        part = slice(k * length, (k + 1) * length)
        turned[part, :] = lax.dot_general(
            eye, table[:, part], NT, preferred_element_type=f32
        ).astype(bf16)

    site_iota = lax.broadcasted_iota(jnp.int32, (length, chains), 0)
    group_iota = lax.broadcasted_iota(jnp.int32, (groups, chains), 0)
    main_iota = lax.broadcasted_iota(jnp.int32, (main, chains), 0)
    extra_iota = lax.broadcasted_iota(jnp.int32, (block - main, chains), 0)

    def place_of(p):
        return ((p % inner) ^ w, (p // inner - z + outer) % outer)

    for r in range(slots):
        slot = slot_ref[r : r + 1, :]
        p = slot // capacity
        s = slot % capacity
        m, k = place_of(p)
        pick = jnp.where(site_iota == s, 1.0, 0.0).astype(bf16)
        looked = jnp.dot(names, pick, preferred_element_type=f32)
        row = jnp.sum(
            jnp.where(group_iota == m * outer + k, looked, 0.0), axis=0, keepdims=True
        )
        row = row.astype(jnp.int32)
        live = row >= 0
        y = row % plan.size_y
        x = row // plan.size_y
        first = jnp.where(live, m * block + k * rows + row, -1)
        m, k = place_of((p + 1) % groups)
        above = m * block + k * extra + x
        m, k = place_of((p + groups - 1) % groups)
        below = m * block + k * extra + plan.size_x + x
        second = jnp.where(y == plan.size_y - 1, above, jnp.where(y == 0, below, -1))
        second = jnp.where(live, second, -1)
        lanes = slice(r * chains, (r + 1) * chains)
        for m in range(inner):
            base = m * block
            onehot[base : base + main, lanes] = jnp.where(
                main_iota == first - base, 1.0, 0.0
            ).astype(bf16)
            onehot[base + main : base + block, lanes] = jnp.where(
                extra_iota == second - base, 1.0, 0.0
            ).astype(bf16)

    picked = jnp.dot(turned[...], onehot[...], preferred_element_type=f32).astype(bf16)
    near = lax.broadcasted_iota(jnp.int32, (length, length), 0)
    near = near - lax.broadcasted_iota(jnp.int32, (length, length), 1)
    around = (near == 1) | (near == -1) | (near == length - 1) | (near == 1 - length)
    kernel = jnp.where(near == 0, 0.5, jnp.where(around, 0.25, 0.0)).astype(bf16)
    for k in range(3):
        part = slice(k * length, (k + 1) * length)
        smooth[part, :] = jnp.dot(kernel, picked[part], preferred_element_type=f32)

    for r in range(slots):
        for octet in range(per_slot // 8):
            for tile in range(chains // 128):
                at = slice(r * per_slot + octet * 8, r * per_slot + octet * 8 + 8)
                lanes = slice(tile * 128, tile * 128 + 128)
                wide = slice(r * chains + tile * 128, r * chains + tile * 128 + 128)
                site = site_ref[at, lanes]
                inside = site & 7
                which = site >> 3
                for k in range(3):
                    value = jnp.zeros((8, 128), f32)
                    for t in range(length // 8):
                        rows8 = slice(k * length + t * 8, k * length + t * 8 + 8)
                        got = jnp.take_along_axis(
                            smooth[rows8, wide], inside, axis=0, mode="promise_in_bounds"
                        )
                        value = jnp.where(which == t, got, value)
                    velocity[k, at, lanes] = value

    stretch = None
    for k in range(3):
        bond = pos_ref[k, 1:, :] - pos_ref[k, : beads - 1, :]
        part = jnp.sum(bond * bond, axis=0, keepdims=True)
        stretch = part if stretch is None else stretch + part
    stretch = stretch / (beads - 1)
    stiffness = SPRING / (1.0 - stretch / MAX_STRETCH)
    damping = 1.0 / (1.0 + spectrum_ref[...] * stiffness)
    basis = basis_ref[...]
    for k in range(3):
        amps = jnp.dot(
            basis, pos_ref[k] + velocity[k], precision=highest, preferred_element_type=f32
        )
        moved = lax.dot_general(
            basis,
            amps * damping,
            (((0,), (0,)), ((), ())),
            precision=highest,
            preferred_element_type=f32,
        )
        moved_ref[k] = moved
        force[k] = (moved - pos_ref[k]) - velocity[k]

    for copy in loads:
        copy.wait()
    brick = lax.axis_index("brick")
    chain_iota = lax.broadcasted_iota(jnp.int32, (1, chains), 1)
    leaving = list_ref.shape[1]
    for i, out in enumerate((stay_ref, leave_ref)):
        target = brick ^ i
        chosen = []
        for s in range(leaving):
            number = jnp.where(s < live_ref[target], list_ref[target, s], -1)
            chosen.append(jnp.where(chain_iota == number, 1.0, 0.0))
        chosen = jnp.concatenate(chosen, axis=0)
        for k in range(3):
            out[:, k * beads : (k + 1) * beads] = lax.dot_general(
                chosen, moved_ref[k], NT, precision=highest, preferred_element_type=f32
            )

    step = 32
    step_iota = lax.broadcasted_iota(jnp.int32, (step, 128), 0)
    for r in range(slots):
        for tile in range(chains // 128):
            lanes = slice(tile * 128, tile * 128 + 128)
            wide = slice(r * chains + tile * 128, r * chains + tile * 128 + 128)
            for start in range(0, length, step):
                parts = [jnp.zeros((step, 128), f32) for _ in range(3)]
                for j in range(per_slot):
                    at = slice(r * per_slot + j, r * per_slot + j + 1)
                    here = step_iota == site_ref[at, lanes] - start
                    for k in range(3):
                        parts[k] = parts[k] + jnp.where(here, force[k, at, lanes], 0.0)
                for k in range(3):
                    out = slice(k * length + start, k * length + start + step)
                    spread[out, wide] = parts[k].astype(bf16)

    sums[...] = lax.dot_general(onehot[...], spread[...], NT, preferred_element_type=f32)
    own_ref[...] = sums[:block, :]
    for m in range(1, inner):
        send_refs[m - 1][...] = sums[m * block : (m + 1) * block, :].astype(bf16)


def sum_kernel(plan, own_ref, *refs):
    came_refs = refs[: plan.inner - 1]
    kept_ref, *send_refs = refs[plan.inner - 1 :]
    rows, extra, main = plan.rows, plan.extra, plan.main
    spare = plan.stride - rows - extra
    tails = own_ref[main:, :]
    for came in came_refs:
        tails = tails + came[main:, :].astype(f32)
    for k, out in enumerate([kept_ref] + send_refs):
        part = slice(k * rows, (k + 1) * rows)
        value = own_ref[part, :]
        for came in came_refs:
            value = value + came[part, :].astype(f32)
        out[:rows, :] = value.astype(out.dtype)
        tail = tails[k * extra : (k + 1) * extra]
        if spare:
            tail = jnp.concatenate([tail, jnp.zeros((spare, tail.shape[1]), f32)], axis=0)
        out[rows:, :] = tail.astype(out.dtype)


def equilibrium(i, density, velocity, square):
    projected = None
    for k in range(3):
        sign = VECTORS[i][k]
        if sign == 0:
            continue
        term = velocity[k] if sign > 0 else -velocity[k]
        projected = term if projected is None else projected + term
    if projected is None:
        return density * (1.0 - 1.5 * square)
    return density * (1.0 + 3.0 * projected + 4.5 * projected * projected - 1.5 * square)


def relax(i, value, state):
    return value - (value - equilibrium(i, *state)) / TAU_RELAX


def shifted(i, value, edge):
    _, shift_y, shift_z = VECTORS[i]
    size_y, length = value.shape
    if shift_y != 0:
        y_iota = lax.broadcasted_iota(jnp.int32, value.shape, 0)
        value = pltpu.roll(value, shift_y % size_y, axis=0)
        edge = jnp.broadcast_to(edge, value.shape)
        value = jnp.where(y_iota == (0 if shift_y > 0 else size_y - 1), edge, value)
    if shift_z != 0:
        value = pltpu.roll(value, shift_z % length, axis=1)
    return value


def cross_kernel(plan, pop_ref, sites_ref, *refs):
    kept_ref = refs[0]
    came_refs = refs[1 : plan.outer]
    low_ref, high_ref, send_ref, state_ref, edge_ref = refs[plan.outer :]
    length = pop_ref.shape[3]
    size_x, size_y, rows = plan.size_x, plan.size_y, plan.rows
    total = kept_ref[...]
    for came in came_refs:
        total = total + came[...].astype(f32)
    force = []
    for k in range(3):
        value = total[:, k * length : (k + 1) * length]
        near = pltpu.roll(value, 1, axis=1) + pltpu.roll(value, length - 1, axis=1)
        force.append(0.5 * value + 0.25 * near)

    def flow(density, momentum, field):
        velocity = [(momentum[k] + TAU_RELAX * field[k]) / density for k in range(3)]
        square = velocity[0] * velocity[0] + velocity[1] * velocity[1] + velocity[2] * velocity[2]
        return (density, velocity, square)

    edges = {}
    for side, (ref, moves) in enumerate(((low_ref, MOVES_UP), (high_ref, MOVES_DOWN))):
        at = len(moves)
        first = rows + side * size_x
        state = flow(
            ref[at],
            [ref[at + 1], ref[at + 2], ref[at + 3]],
            [force[k][first : first + size_x] for k in range(3)],
        )
        for slot, i in enumerate(moves):
            edges[i] = relax(i, ref[slot], state)
            edge_ref[i] = edges[i]

    for x in range(size_x):
        part = slice(x * size_y, (x + 1) * size_y)
        state = flow(
            sites_ref[0, part, :],
            [sites_ref[k + 1, part, :] for k in range(3)],
            [force[k][part] for k in range(3)],
        )
        density, velocity, square = state
        for slot, value in enumerate([density] + velocity + [square]):
            state_ref[slot, part, :] = value
        for slot, i in enumerate(CROSSING):
            if not 0 <= x + VECTORS[i][0] < size_x:
                edge = edges[i][x : x + 1] if i in edges else None
                send_ref[slot] = shifted(i, relax(i, pop_ref[i, x], state), edge)


def collide_kernel(plan, pop_ref, state_ref, edge_ref, read_ref):
    size_x, size_y = plan.size_x, plan.size_y
    for x in range(size_x):
        part = slice(x * size_y, (x + 1) * size_y)
        state = (
            state_ref[0, part, :],
            [state_ref[k + 1, part, :] for k in range(3)],
            state_ref[4, part, :],
        )
        for i in range(DIRECTIONS):
            target = x + VECTORS[i][0]
            if 0 <= target < size_x:
                edge = edge_ref[i, x : x + 1, :]
                read_ref[i, target] = shifted(i, relax(i, pop_ref[i, x], state), edge)


def merge_kernel(plan, came_ref, part_ref, read_ref, sem):
    del part_ref
    copies = []
    for slot, i in enumerate(CROSSING):
        target = 0 if VECTORS[i][0] > 0 else plan.size_x - 1
        copies.append(
            pltpu.make_async_copy(came_ref.at[slot], read_ref.at[i, target], sem.at[slot])
        )
    for copy in copies:
        copy.start()
    for copy in copies:
        copy.wait()


def local(
    populations,
    positions,
    bead_site,
    chain_slots,
    send_rows,
    send_count,
    migrate_list,
    migrate_count,
):
    size_x, size_y, length = populations.shape[1:]
    groups = lax.axis_size("chain")
    bricks = lax.axis_size("brick")
    capacity = send_rows.shape[-1]
    plan = Plan(groups, size_x * size_y, size_y)
    inner, outer = plan.inner, plan.outer
    beads, chains = positions.shape[3:]
    slots = chain_slots.shape[2]
    shape = jax.ShapeDtypeStruct
    width = 3 * length
    edge = shape((len(MOVES_UP) + 4, size_x, length), f32)

    params = pltpu.CompilerParams
    first = pl.pallas_call(
        functools.partial(moment_kernel, plan),
        out_shape=[shape((plan.stride, width), bf16)] * outer
        + [edge, edge, shape((4, plan.rows, length), f32), shape((slots, chains), jnp.int32)],
        in_specs=[HBM] * 4,
        out_specs=[VMEM] * (outer + 4),
        scratch_shapes=[
            pltpu.VMEM(populations.shape, f32),
            pltpu.VMEM((groups, capacity), jnp.int32),
            pltpu.SMEM((groups,), jnp.int32),
            pltpu.SemaphoreType.DMA((size_x + 3,)),
        ],
        compiler_params=params(vmem_limit_bytes=6 << 20),
        name="moments",
    )(populations, send_rows[0, 0], send_count[0, 0], chain_slots[0, 0])
    msgs, (edge_up, edge_down, sites, slot_list) = first[:outer], first[outer:]
    parts = [msgs[0]]
    for k in range(1, outer):
        parts.append(lax.ppermute(msgs[k], "chain", plan.outer_shift(-k)))
    near = pl.pallas_call(
        functools.partial(pack_kernel, plan),
        out_shape=shape((plan.block, width), bf16),
        in_specs=[VMEM] * outer,
        out_specs=VMEM,
        compiler_params=params(vmem_limit_bytes=4 << 20),
        name="pack",
    )(*parts)
    blocks = [near]
    for m in range(1, inner):
        blocks.append(lax.ppermute(blocks[0], "chain", plan.inner_swap(m)))
    up = [(i, (i + 1) % groups) for i in range(groups)]
    down = [(j, i) for i, j in up]
    low = lax.ppermute(edge_up, "chain", up)
    high = lax.ppermute(edge_down, "chain", down)
    blocks, low, high = lax.optimization_barrier((blocks, low, high))

    basis, spectrum = rouse_tables(beads)
    total = inner * plan.block
    leaving = migrate_list.shape[-1]
    second = pl.pallas_call(
        functools.partial(chain_kernel, plan, capacity),
        out_shape=[shape((plan.block, width), f32)]
        + [shape((plan.block, width), bf16)] * (inner - 1)
        + [shape((3, beads, chains), f32)]
        + [shape((leaving, 3 * beads), f32)] * 2,
        in_specs=[VMEM] * (inner + 3) + [HBM, HBM] + [VMEM, VMEM],
        out_specs=[VMEM] * (inner + 3),
        scratch_shapes=[
            pltpu.VMEM((total, width), bf16),
            pltpu.VMEM((width, total), bf16),
            pltpu.VMEM((total, slots * chains), bf16),
            pltpu.VMEM((width, slots * chains), f32),
            pltpu.VMEM((3, beads, chains), f32),
            pltpu.VMEM((3, beads, chains), f32),
            pltpu.VMEM((width, slots * chains), bf16),
            pltpu.VMEM((total, width), f32),
            pltpu.SMEM((bricks, leaving), jnp.int32),
            pltpu.SMEM((bricks,), jnp.int32),
            pltpu.SemaphoreType.DMA((2,)),
        ],
        compiler_params=params(vmem_limit_bytes=(12 << 20) + total * 8192),
        name="chains",
    )(
        *blocks,
        positions[0, 0],
        bead_site[0, 0],
        slot_list,
        migrate_list[0, 0],
        migrate_count[0, 0],
        basis,
        spectrum,
    )
    own, sends = second[0], second[1:inner]
    moved, stay, leave = second[inner:]
    came = []
    for m in range(1, inner):
        came.append(lax.ppermute(sends[m - 1], "chain", plan.inner_swap(m)))
    swap = [(i, (i + 1) % bricks) for i in range(bricks)]
    arrived = lax.ppermute(leave, "brick", swap)
    came, arrived = lax.optimization_barrier((came, arrived))
    kept, *outgoing = pl.pallas_call(
        functools.partial(sum_kernel, plan),
        out_shape=[shape((plan.stride, width), f32)]
        + [shape((plan.stride, width), bf16)] * (outer - 1),
        in_specs=[VMEM] * inner,
        out_specs=[VMEM] * outer,
        compiler_params=params(vmem_limit_bytes=8 << 20),
        name="sums",
    )(own, *came)
    came = []
    for k in range(1, outer):
        came.append(lax.ppermute(outgoing[k - 1], "chain", plan.outer_shift(k)))
    crossing, state, edges = pl.pallas_call(
        functools.partial(cross_kernel, plan),
        out_shape=[
            shape((len(CROSSING), size_y, length), f32),
            shape((5, plan.rows, length), f32),
            shape((DIRECTIONS, size_x, length), f32),
        ],
        in_specs=[VMEM] * (outer + 4),
        out_specs=[VMEM] * 3,
        compiler_params=params(vmem_limit_bytes=6 << 20),
        name="cross",
    )(populations, sites, kept, *came, low, high)
    crossed = lax.ppermute(crossing, "brick", swap)
    partial = pl.pallas_call(
        functools.partial(collide_kernel, plan),
        out_shape=shape(populations.shape, f32),
        in_specs=[VMEM] * 3,
        out_specs=VMEM,
        compiler_params=params(vmem_limit_bytes=6 << 20),
        name="collide",
    )(populations, state, edges)
    read = pl.pallas_call(
        functools.partial(merge_kernel, plan),
        out_shape=shape(populations.shape, f32),
        in_specs=[VMEM, ANY],
        out_specs=ANY,
        scratch_shapes=[pltpu.SemaphoreType.DMA((len(CROSSING),))],
        input_output_aliases={1: 0},
        compiler_params=params(vmem_limit_bytes=4 << 20),
        name="merge",
    )(crossed, partial)
    here = lax.axis_index("brick")
    stay = stay.reshape(1, -1)
    arrived = arrived.reshape(1, -1)
    arrivals = jnp.where(
        here == 0,
        jnp.concatenate([stay, arrived], axis=0),
        jnp.concatenate([arrived, stay], axis=0),
    )
    return (read, moved[None, None], arrivals[None, None])


def solution(mesh):
    placed = (
        P(None, "brick", "chain", None),
        P("brick", "chain", None, None, None),
        P("brick", "chain", None, None),
        P("brick", "chain", None, None),
        P("brick", "chain", None, None),
        P("brick", "chain", None),
        P("brick", "chain", None, None),
        P("brick", "chain", None),
    )

    return jax.shard_map(
        local,
        mesh=mesh,
        in_specs=placed,
        out_specs=(
            P(None, "brick", "chain", None),
            P("brick", "chain", None, None, None),
            P("brick", "chain", None, None),
        ),
        check_vma=False,
    )
```

```python
import functools
import math

import jax
import jax.numpy as jnp
import numpy as np
from jax import lax
from jax.experimental import pallas as pl
from jax.experimental.pallas import tpu as pltpu
from jax.sharding import PartitionSpec as P

LATTICE_VECTORS = np.array(
    [
        [0, 0, 0],
        [1, 0, 0],
        [-1, 0, 0],
        [0, 1, 0],
        [0, -1, 0],
        [0, 0, 1],
        [0, 0, -1],
        [1, 1, 0],
        [-1, -1, 0],
        [1, -1, 0],
        [-1, 1, 0],
        [1, 0, 1],
        [-1, 0, -1],
        [1, 0, -1],
        [-1, 0, 1],
        [0, 1, 1],
        [0, -1, -1],
        [0, 1, -1],
        [0, -1, 1],
    ],
    np.int32,
)
WEIGHT_TABLE = [1.0 / 3.0] + [1.0 / 18.0] * 6 + [1.0 / 36.0] * 12
DIRECTIONS = len(WEIGHT_TABLE)
VECTORS = [tuple(int(v) for v in row) for row in LATTICE_VECTORS]
MOVES_UP = [i for i in range(DIRECTIONS) if VECTORS[i][1] == 1]
MOVES_DOWN = [i for i in range(DIRECTIONS) if VECTORS[i][1] == -1]
CROSSING = [i for i in range(DIRECTIONS) if VECTORS[i][0] != 0]
TAU_RELAX = 0.8
SPRING = 0.5
MAX_STRETCH = 4.0
f32 = jnp.float32
bf16 = jnp.bfloat16
highest = lax.Precision.HIGHEST
NT = (((1,), (1,)), ((), ()))
VMEM = pl.BlockSpec(memory_space=pltpu.VMEM)
SMEM = pl.BlockSpec(memory_space=pltpu.SMEM)
ANY = pl.BlockSpec(memory_space=pl.ANY)
HBM = pl.BlockSpec(memory_space=pltpu.HBM)


class Plan:
    def __init__(self, groups, rows, size_y, length):
        self.length = length
        self.groups = groups
        self.outer = 4
        self.inner = groups // self.outer
        self.rows = rows
        self.size_y = size_y
        self.size_x = rows // size_y
        self.extra = max(self.inner, 2 * self.size_x)
        self.stride = (rows + self.extra + 7) // 8 * 8
        self.main = self.outer * rows
        self.block = (self.main + self.outer * self.extra + 15) // 16 * 16

    def outer_swap(self, k):
        z_count, w_count = self.outer, self.inner
        return [
            (z * w_count + w, (z ^ k) * w_count + w)
            for z in range(z_count)
            for w in range(w_count)
        ]

    def inner_swap(self, m):
        z_count, w_count = self.outer, self.inner
        return [
            (z * w_count + w, z * w_count + (w ^ m))
            for z in range(z_count)
            for w in range(w_count)
        ]


def rouse_tables(bead_count):
    mode = np.arange(bead_count, dtype=np.float64)
    basis = math.sqrt(2.0 / bead_count) * np.cos(
        math.pi * mode[:, None] * (mode[None, :] + 0.5) / bead_count
    )
    basis[0] = math.sqrt(1.0 / bead_count)
    spectrum = 4.0 * np.sin(math.pi * mode / (2.0 * bead_count)) ** 2
    return (basis.astype(np.float32), spectrum.astype(np.float32)[:, None])


def weighted_sums(get):
    density = None
    momentum = [None, None, None]
    for i in range(DIRECTIONS):
        value = get(i) * np.float32(WEIGHT_TABLE[i])
        density = value if density is None else density + value
        for k in range(3):
            sign = VECTORS[i][k]
            if sign == 0:
                continue
            term = value if sign > 0 else -value
            momentum[k] = term if momentum[k] is None else momentum[k] + term
    return (density, momentum)


def moment_kernel(plan, pop_hbm, rows_hbm, count_hbm, slots_hbm, list_hbm, live_hbm, *outs):
    msg_refs = outs[: plan.outer]
    up_ref, down_ref, state_ref, slots_ref, leave_ref = outs[plan.outer : plan.outer + 5]
    pop_ref, rows_ref, count_ref, list_ref, live_ref, sem = outs[plan.outer + 5 :]
    length = pop_ref.shape[3]
    size_x, size_y = plan.size_x, plan.size_y
    loads = [
        pltpu.make_async_copy(pop_hbm.at[:, x], pop_ref.at[:, x], sem.at[x])
        for x in range(size_x)
    ]
    others = [
        pltpu.make_async_copy(rows_hbm, rows_ref, sem.at[size_x]),
        pltpu.make_async_copy(count_hbm, count_ref, sem.at[size_x + 1]),
        pltpu.make_async_copy(slots_hbm, slots_ref, sem.at[size_x + 2]),
        pltpu.make_async_copy(list_hbm, list_ref, sem.at[size_x + 3]),
        pltpu.make_async_copy(live_hbm, live_ref, sem.at[size_x + 4]),
    ]
    for copy in loads + others:
        copy.start()
    for x in range(size_x):
        loads[x].wait()
        density, momentum = weighted_sums(lambda i: pop_ref[i, x])
        first = slice(x * size_y, (x + 1) * size_y)
        for slot, value in enumerate([density] + momentum):
            state_ref[slot, first, :] = value
        for k in range(3):
            velocity = (momentum[k] / density).astype(bf16)
            for msg in msg_refs:
                msg[first, k * length : (k + 1) * length] = velocity
        for out, moves, row in ((up_ref, MOVES_UP, size_y - 1), (down_ref, MOVES_DOWN, 0)):
            for slot, i in enumerate(moves):
                out[slot, x : x + 1, :] = pop_ref[i, x, row : row + 1, :]
            at = len(moves)
            for slot, value in enumerate([density] + momentum):
                out[at + slot, x : x + 1, :] = value[row : row + 1]
    for copy in others:
        copy.wait()
    brick = lax.axis_index("brick")
    leaving = list_ref.shape[1]
    for i in range(list_ref.shape[0]):
        target = brick ^ i
        for s in range(leaving):
            number = jnp.where(s < live_ref[target], list_ref[target, s], -1)
            at = i * leaving + s
            leave_ref[at : at + 1, :] = jnp.full((1, length), number, jnp.int32)
    me = lax.axis_index("chain")
    z = me // plan.inner
    w = me % plan.inner
    lane = lax.broadcasted_iota(jnp.int32, (1, length), 1)
    extra = plan.stride - plan.rows
    for k, msg in enumerate(msg_refs):
        tables = []
        for m in range(plan.inner):
            target = (z ^ k) * plan.inner + (w ^ m)
            row = rows_ref[pl.ds(target, 1), :]
            tables.append(jnp.where(lane < count_ref[target], row, -1).astype(f32))
        if extra > plan.inner:
            tables.append(jnp.zeros((extra - plan.inner, length), f32))
        block = jnp.concatenate(tables, axis=0).astype(bf16)
        msg[plan.rows :, :length] = block
        msg[plan.rows :, length:] = jnp.zeros((extra, 2 * length), bf16)


def pack_kernel(plan, *refs):
    part_refs, out_ref = refs[:-1], refs[-1]
    rows, extra = plan.rows, plan.extra
    tails = []
    for k, part in enumerate(part_refs):
        out_ref[k * rows : (k + 1) * rows, :] = part[:rows, :]
        tails.append(part[rows:, :].astype(f32)[:extra])
    spare = plan.block - plan.main - plan.outer * extra
    if spare:
        tails.append(jnp.zeros((spare, out_ref.shape[1]), f32))
    out_ref[plan.main :, :] = jnp.concatenate(tails, axis=0).astype(bf16)


def prepare_kernel(plan, own_ref, pos_ref, site_ref, spectrum_ref, rows_ref, bead_ref, damp_ref):
    rows_ref[...] = own_ref[...]
    beads, chains = site_ref.shape
    per_slot = beads * plan.length // bead_ref.shape[0]
    step = 32
    step_iota = lax.broadcasted_iota(jnp.int32, (step, 128), 0)
    for r in range(beads // per_slot):
        for tile in range(chains // 128):
            lanes = slice(tile * 128, tile * 128 + 128)
            for start in range(0, plan.length, step):
                bead = jnp.full((step, 128), -1, jnp.int32)
                for j in range(per_slot):
                    at = slice(r * per_slot + j, r * per_slot + j + 1)
                    bead = jnp.where(step_iota == site_ref[at, lanes] - start, j, bead)
                first = r * plan.length + start
                bead_ref[first : first + step, lanes] = bead

    stretch = None
    for k in range(3):
        bond = pos_ref[k, 1:, :] - pos_ref[k, : beads - 1, :]
        part = jnp.sum(bond * bond, axis=0, keepdims=True)
        stretch = part if stretch is None else stretch + part
    stretch = stretch / (beads - 1)
    stiffness = SPRING / (1.0 - stretch / MAX_STRETCH)
    damp_ref[...] = 1.0 / (1.0 + spectrum_ref[...] * stiffness)


def one_hot(condition):
    return jnp.where(condition, 1.0, 0.0).astype(bf16)


def place_of(plan, p):
    me = lax.axis_index("chain")
    z = me // plan.inner
    w = me % plan.inner
    return ((p % plan.inner) ^ w, (p // plan.inner) ^ z)


def pick_block(plan, capacity, m, block_ref, slot_ref, table, hot_ref):
    outer, rows, main, extra, length = plan.outer, plan.rows, plan.main, plan.extra, plan.length
    slots, chains = slot_ref.shape
    tail = block_ref[main:, :length].astype(f32)
    names = [tail[k * extra + m : k * extra + m + 1] for k in range(outer)]
    names += [jnp.zeros((8 - outer, length), f32)] if outer < 8 else []
    names = jnp.concatenate(names, axis=0).astype(bf16)
    eye = lax.broadcasted_iota(jnp.int32, (length, length), 0)
    eye = one_hot(eye == lax.broadcasted_iota(jnp.int32, (length, length), 1))
    for k in range(3):
        part = slice(k * length, (k + 1) * length)
        table[part, :] = lax.dot_general(
            eye, block_ref[:main, part], NT, preferred_element_type=f32
        ).astype(bf16)
    site_iota = lax.broadcasted_iota(jnp.int32, (length, chains), 0)
    outer_iota = lax.broadcasted_iota(jnp.int32, (names.shape[0], chains), 0)
    main_iota = lax.broadcasted_iota(jnp.int32, (main, chains), 0)
    found = []
    for r in range(slots):
        slot = slot_ref[r : r + 1, :]
        which, k = place_of(plan, slot // capacity)
        pick = one_hot(site_iota == slot % capacity)
        looked = jnp.dot(names, pick, preferred_element_type=f32)
        row = jnp.sum(jnp.where(outer_iota == k, looked, 0.0), axis=0, keepdims=True)
        row = jnp.where(which == m, row.astype(jnp.int32), -1)
        first = jnp.where(row >= 0, k * rows + row, -1)
        hot_ref[:, r * chains : (r + 1) * chains] = one_hot(main_iota == first)
        found.append(row)
    picked = jnp.dot(table[...], hot_ref[...], preferred_element_type=f32).astype(bf16)
    return (picked, jnp.concatenate(found, axis=0))


def pick_kernel(plan, capacity, m, block_ref, slot_ref, *refs):
    before, (hot_ref, picked_ref, row_ref, table) = refs[:-4], refs[-4:]
    picked, row = pick_block(plan, capacity, m, block_ref, slot_ref, table, hot_ref)
    if before:
        picked = picked + before[0][...]
        row = jnp.maximum(row, before[1][...])
    picked_ref[...] = picked
    row_ref[...] = row


def chain_kernel(plan, capacity, *refs):
    inner, main, block, length = plan.inner, plan.main, plan.block, plan.length
    hot_refs, refs = list(refs[: inner - 1]), refs[inner - 1 :]
    block_ref, slot_ref, before_ref, row_ref, pos_ref, site_ref = refs[:6]
    bead_ref, damp_ref, basis_ref = refs[6:9]
    send_refs, refs = refs[9 : 8 + inner], refs[8 + inner :]
    moved_ref, spread, extras, table, last_hot, smooth, velocity, force = refs
    hot_refs.append(last_hot)
    slots, chains = slot_ref.shape
    beads = pos_ref.shape[1]
    per_slot = beads // slots
    groups = plan.groups
    tail = block - main

    picked, row = pick_block(plan, capacity, inner - 1, block_ref, slot_ref, table, last_hot)
    picked = picked + before_ref[...]
    row = jnp.maximum(row, row_ref[...])
    near = lax.broadcasted_iota(jnp.int32, (length, length), 0)
    near = near - lax.broadcasted_iota(jnp.int32, (length, length), 1)
    around = (near == 1) | (near == -1) | (near == length - 1) | (near == 1 - length)
    kernel = jnp.where(near == 0, 0.5, jnp.where(around, 0.25, 0.0)).astype(bf16)
    for k in range(3):
        part = slice(k * length, (k + 1) * length)
        smooth[part, :] = jnp.dot(kernel, picked[part], preferred_element_type=f32)

    p = slot_ref[...] // capacity
    y = row % plan.size_y
    x = row // plan.size_y
    m, k = place_of(plan, (p + 1) % groups)
    above = m * tail + k * plan.extra + x
    m, k = place_of(plan, (p + groups - 1) % groups)
    below = m * tail + k * plan.extra + plan.size_x + x
    second = jnp.where(y == plan.size_y - 1, above, jnp.where(y == 0, below, -1))
    second = jnp.where(row >= 0, second, -1)
    extra_iota = lax.broadcasted_iota(jnp.int32, (inner * tail, chains), 0)
    for r in range(slots):
        extras[:, r * chains : (r + 1) * chains] = one_hot(extra_iota == second[r : r + 1])

    for r in range(slots):
        for octet in range(per_slot // 8):
            for tile in range(chains // 128):
                at = slice(r * per_slot + octet * 8, r * per_slot + octet * 8 + 8)
                lanes = slice(tile * 128, tile * 128 + 128)
                wide = slice(r * chains + tile * 128, r * chains + tile * 128 + 128)
                site = site_ref[at, lanes]
                inside = site & 7
                which = site >> 3
                for k in range(3):
                    value = jnp.zeros((8, 128), f32)
                    for t in range(length // 8):
                        rows8 = slice(k * length + t * 8, k * length + t * 8 + 8)
                        got = jnp.take_along_axis(
                            smooth[rows8, wide], inside, axis=0, mode="promise_in_bounds"
                        )
                        value = jnp.where(which == t, got, value)
                    velocity[k, at, lanes] = value

    damping = damp_ref[...]
    basis = basis_ref[...]
    for k in range(3):
        amps = jnp.dot(
            basis, pos_ref[k] + velocity[k], precision=highest, preferred_element_type=f32
        )
        moved = lax.dot_general(
            basis,
            amps * damping,
            (((0,), (0,)), ((), ())),
            precision=highest,
            preferred_element_type=f32,
        )
        moved_ref[k] = moved
        force[k] = (moved - pos_ref[k]) - velocity[k]

    step = 32
    octets = per_slot // 8
    for r in range(slots):
        for tile in range(chains // 128):
            lanes = slice(tile * 128, tile * 128 + 128)
            wide = slice(r * chains + tile * 128, r * chains + tile * 128 + 128)
            mine = slice(r * per_slot, (r + 1) * per_slot)
            site = site_ref[mine, lanes]
            joint = [jnp.zeros((per_slot, 128), f32) for _ in range(3)]
            for j in range(per_slot):
                at = slice(r * per_slot + j, r * per_slot + j + 1)
                same = site == site_ref[at, lanes]
                for k in range(3):
                    joint[k] = joint[k] + jnp.where(same, force[k, at, lanes], 0.0)
            for start in range(0, length, step):
                first = r * length + start
                bead = bead_ref[first : first + step, lanes]
                inside = bead & 7
                which = bead >> 3
                for k in range(3):
                    out = slice(k * length + start, k * length + start + step)
                    value = jnp.zeros((step, 128), f32)
                    for octet in range(octets):
                        source = joint[k][octet * 8 : octet * 8 + 8]
                        got = jnp.concatenate(
                            [
                                jnp.take_along_axis(
                                    source,
                                    inside[t : t + 8],
                                    axis=0,
                                    mode="promise_in_bounds",
                                )
                                for t in range(0, step, 8)
                            ],
                            axis=0,
                        )
                        value = jnp.where(which == octet, got, value)
                    spread[out, wide] = value.astype(bf16)

    sides = lax.dot_general(extras[...], spread[...], NT, preferred_element_type=f32)
    for m in range(1, inner):
        send_refs[m - 1][:main, :] = lax.dot_general(
            hot_refs[m][...], spread[...], NT, preferred_element_type=f32
        ).astype(bf16)
        send_refs[m - 1][main:, :] = sides[m * tail : (m + 1) * tail].astype(bf16)


def own_kernel(plan, hot_ref, extras_ref, spread_ref, moved_ref, number_ref, own_ref, stay_ref, leave_ref):
    main = plan.main
    tail = plan.block - main
    beads, chains = moved_ref.shape[1:]
    leaving = number_ref.shape[0] // 2
    chain_iota = lax.broadcasted_iota(jnp.int32, (leaving, chains), 1)
    for i, out in enumerate((stay_ref, leave_ref)):
        numbers = number_ref[i * leaving : (i + 1) * leaving, :1]
        chosen = jnp.where(chain_iota == numbers, 1.0, 0.0)
        for k in range(3):
            out[:, k * beads : (k + 1) * beads] = lax.dot_general(
                chosen, moved_ref[k], NT, precision=highest, preferred_element_type=f32
            )
    own_ref[:main, :] = lax.dot_general(
        hot_ref[...], spread_ref[...], NT, preferred_element_type=f32
    )
    own_ref[main:, :] = lax.dot_general(
        extras_ref[:tail, :], spread_ref[...], NT, preferred_element_type=f32
    )


def sum_kernel(plan, own_ref, *refs):
    came_refs = refs[: plan.inner - 1]
    kept_ref, *send_refs = refs[plan.inner - 1 :]
    rows, extra, main = plan.rows, plan.extra, plan.main
    spare = plan.stride - rows - extra
    tails = own_ref[main:, :]
    for came in came_refs:
        tails = tails + came[main:, :].astype(f32)
    for k, out in enumerate([kept_ref] + send_refs):
        part = slice(k * rows, (k + 1) * rows)
        value = own_ref[part, :]
        for came in came_refs:
            value = value + came[part, :].astype(f32)
        out[:rows, :] = value.astype(out.dtype)
        tail = tails[k * extra : (k + 1) * extra]
        if spare:
            tail = jnp.concatenate([tail, jnp.zeros((spare, tail.shape[1]), f32)], axis=0)
        out[rows:, :] = tail.astype(out.dtype)


def equilibrium(i, density, velocity, square):
    projected = None
    for k in range(3):
        sign = VECTORS[i][k]
        if sign == 0:
            continue
        term = velocity[k] if sign > 0 else -velocity[k]
        projected = term if projected is None else projected + term
    if projected is None:
        return density * (1.0 - 1.5 * square)
    return density * (1.0 + 3.0 * projected + 4.5 * projected * projected - 1.5 * square)


def relax(i, value, state):
    return value - (value - equilibrium(i, *state)) / TAU_RELAX


def shifted(i, value, edge):
    _, shift_y, shift_z = VECTORS[i]
    size_y, length = value.shape
    if shift_y != 0:
        y_iota = lax.broadcasted_iota(jnp.int32, value.shape, 0)
        value = pltpu.roll(value, shift_y % size_y, axis=0)
        edge = jnp.broadcast_to(edge, value.shape)
        value = jnp.where(y_iota == (0 if shift_y > 0 else size_y - 1), edge, value)
    if shift_z != 0:
        value = pltpu.roll(value, shift_z % length, axis=1)
    return value


def cross_kernel(plan, pop_ref, sites_ref, *refs):
    kept_ref = refs[0]
    came_refs = refs[1 : plan.outer]
    low_ref, high_ref, send_ref, state_ref, edge_ref = refs[plan.outer :]
    length = pop_ref.shape[3]
    size_x, size_y, rows = plan.size_x, plan.size_y, plan.rows
    total = kept_ref[...]
    for came in came_refs:
        total = total + came[...].astype(f32)
    force = []
    for k in range(3):
        value = total[:, k * length : (k + 1) * length]
        near = pltpu.roll(value, 1, axis=1) + pltpu.roll(value, length - 1, axis=1)
        force.append(0.5 * value + 0.25 * near)

    def flow(density, momentum, field):
        velocity = [(momentum[k] + TAU_RELAX * field[k]) / density for k in range(3)]
        square = velocity[0] * velocity[0] + velocity[1] * velocity[1] + velocity[2] * velocity[2]
        return (density, velocity, square)

    edges = {}
    for side, (ref, moves) in enumerate(((low_ref, MOVES_UP), (high_ref, MOVES_DOWN))):
        at = len(moves)
        first = rows + side * size_x
        state = flow(
            ref[at],
            [ref[at + 1], ref[at + 2], ref[at + 3]],
            [force[k][first : first + size_x] for k in range(3)],
        )
        for slot, i in enumerate(moves):
            edges[i] = relax(i, ref[slot], state)
            edge_ref[i] = edges[i]

    for x in range(size_x):
        part = slice(x * size_y, (x + 1) * size_y)
        state = flow(
            sites_ref[0, part, :],
            [sites_ref[k + 1, part, :] for k in range(3)],
            [force[k][part] for k in range(3)],
        )
        density, velocity, square = state
        for slot, value in enumerate([density] + velocity + [square]):
            state_ref[slot, part, :] = value
        for slot, i in enumerate(CROSSING):
            if not 0 <= x + VECTORS[i][0] < size_x:
                edge = edges[i][x : x + 1] if i in edges else None
                send_ref[slot] = shifted(i, relax(i, pop_ref[i, x], state), edge)


def collide_kernel(plan, pop_ref, state_ref, edge_ref, read_ref):
    size_x, size_y = plan.size_x, plan.size_y
    for x in range(size_x):
        part = slice(x * size_y, (x + 1) * size_y)
        state = (
            state_ref[0, part, :],
            [state_ref[k + 1, part, :] for k in range(3)],
            state_ref[4, part, :],
        )
        for i in range(DIRECTIONS):
            target = x + VECTORS[i][0]
            if 0 <= target < size_x:
                edge = edge_ref[i, x : x + 1, :]
                read_ref[i, target] = shifted(i, relax(i, pop_ref[i, x], state), edge)


def merge_kernel(plan, came_ref, part_ref, read_ref, sem):
    del part_ref
    copies = []
    for slot, i in enumerate(CROSSING):
        target = 0 if VECTORS[i][0] > 0 else plan.size_x - 1
        copies.append(
            pltpu.make_async_copy(came_ref.at[slot], read_ref.at[i, target], sem.at[slot])
        )
    for copy in copies:
        copy.start()
    for copy in copies:
        copy.wait()


def local(
    populations,
    positions,
    bead_site,
    chain_slots,
    send_rows,
    send_count,
    migrate_list,
    migrate_count,
):
    size_x, size_y, length = populations.shape[1:]
    groups = lax.axis_size("chain")
    bricks = lax.axis_size("brick")
    capacity = send_rows.shape[-1]
    plan = Plan(groups, size_x * size_y, size_y, length)
    inner, outer = plan.inner, plan.outer
    beads, chains = positions.shape[3:]
    slots = chain_slots.shape[2]
    shape = jax.ShapeDtypeStruct
    width = 3 * length
    edge = shape((len(MOVES_UP) + 4, size_x, length), f32)
    leaving = migrate_list.shape[-1]

    params = pltpu.CompilerParams
    first = pl.pallas_call(
        functools.partial(moment_kernel, plan),
        out_shape=[shape((plan.stride, width), bf16)] * outer
        + [edge, edge, shape((4, plan.rows, length), f32), shape((slots, chains), jnp.int32)]
        + [shape((bricks * leaving, length), jnp.int32)],
        in_specs=[HBM] * 6,
        out_specs=[VMEM] * (outer + 5),
        scratch_shapes=[
            pltpu.VMEM(populations.shape, f32),
            pltpu.VMEM((groups, capacity), jnp.int32),
            pltpu.SMEM((groups,), jnp.int32),
            pltpu.SMEM((bricks, leaving), jnp.int32),
            pltpu.SMEM((bricks,), jnp.int32),
            pltpu.SemaphoreType.DMA((size_x + 5,)),
        ],
        compiler_params=params(vmem_limit_bytes=62 << 20),
        name="moments",
    )(
        populations,
        send_rows[0, 0],
        send_count[0, 0],
        chain_slots[0, 0],
        migrate_list[0, 0],
        migrate_count[0, 0],
    )
    msgs, (edge_up, edge_down, sites, slot_list, numbers) = first[:outer], first[outer:]
    parts = [msgs[0]]
    for k in range(1, outer):
        parts.append(lax.ppermute(msgs[k], "chain", plan.outer_swap(k)))
    basis, spectrum = rouse_tables(beads)
    own_rows, bead, damping = pl.pallas_call(
        functools.partial(prepare_kernel, plan),
        out_shape=[
            shape((plan.stride, width), bf16),
            shape((slots * length, chains), jnp.int32),
            shape((beads, chains), f32),
        ],
        in_specs=[VMEM] * 4,
        out_specs=[VMEM] * 3,
        compiler_params=params(vmem_limit_bytes=6 << 20),
        name="prepare",
    )(msgs[0], positions[0, 0], bead_site[0, 0], spectrum)
    near = pl.pallas_call(
        functools.partial(pack_kernel, plan),
        out_shape=shape((plan.block, width), bf16),
        in_specs=[VMEM] * outer,
        out_specs=VMEM,
        compiler_params=params(vmem_limit_bytes=4 << 20),
        name="pack",
    )(own_rows, *parts[1:])
    blocks = [near]
    for m in range(1, inner):
        blocks.append(lax.ppermute(near, "chain", plan.inner_swap(m)))
    up = [(i, (i + 1) % groups) for i in range(groups)]
    down = [(j, i) for i, j in up]
    low = lax.ppermute(edge_up, "chain", up)

    items = slots * chains
    hot = shape((plan.main, items), bf16)
    hots, before = [], []
    for m in range(inner - 1):
        one, *before = pl.pallas_call(
            functools.partial(pick_kernel, plan, capacity, m),
            out_shape=[hot, shape((width, items), bf16), shape((slots, chains), jnp.int32)],
            in_specs=[VMEM] * (2 + len(before)),
            out_specs=[VMEM] * 3,
            scratch_shapes=[pltpu.VMEM((width, plan.main), bf16)],
            compiler_params=params(vmem_limit_bytes=8 << 20),
            name="pick",
        )(blocks[m], slot_list, *before)
        hots.append(one)
    second = pl.pallas_call(
        functools.partial(chain_kernel, plan, capacity),
        out_shape=[shape((plan.block, width), bf16)] * (inner - 1)
        + [
            shape((3, beads, chains), f32),
            shape((width, items), bf16),
            shape((inner * (plan.block - plan.main), items), bf16),
        ],
        in_specs=[VMEM] * (inner + 8),
        out_specs=[VMEM] * (inner + 2),
        scratch_shapes=[
            pltpu.VMEM((width, plan.main), bf16),
            pltpu.VMEM((plan.main, items), bf16),
            pltpu.VMEM((width, items), f32),
            pltpu.VMEM((3, beads, chains), f32),
            pltpu.VMEM((3, beads, chains), f32),
        ],
        compiler_params=params(vmem_limit_bytes=16 << 20),
        name="chains",
    )(
        *hots,
        blocks[inner - 1],
        slot_list,
        *before,
        positions[0, 0],
        bead_site[0, 0],
        bead,
        damping,
        basis,
    )
    sends, (moved, spread, extras) = second[: inner - 1], second[inner - 1 :]
    came = []
    for m in range(1, inner):
        came.append(lax.ppermute(sends[m - 1], "chain", plan.inner_swap(m)))
    own, stay, leave = pl.pallas_call(
        functools.partial(own_kernel, plan),
        out_shape=[shape((plan.block, width), f32)]
        + [shape((leaving, 3 * beads), f32)] * 2,
        in_specs=[VMEM] * 5,
        out_specs=[VMEM] * 3,
        compiler_params=params(vmem_limit_bytes=8 << 20),
        name="own",
    )(hots[0], extras, spread, moved, numbers)
    swap = [(i, (i + 1) % bricks) for i in range(bricks)]
    arrived = lax.ppermute(leave, "brick", swap)
    high = lax.ppermute(edge_down, "chain", down)
    came, arrived = lax.optimization_barrier((came, arrived))
    kept, *outgoing = pl.pallas_call(
        functools.partial(sum_kernel, plan),
        out_shape=[shape((plan.stride, width), f32)]
        + [shape((plan.stride, width), bf16)] * (outer - 1),
        in_specs=[VMEM] * inner,
        out_specs=[VMEM] * outer,
        compiler_params=params(vmem_limit_bytes=8 << 20),
        name="sums",
    )(own, *came)
    came = []
    for k in range(1, outer):
        came.append(lax.ppermute(outgoing[k - 1], "chain", plan.outer_swap(k)))
    crossing, state, edges = pl.pallas_call(
        functools.partial(cross_kernel, plan),
        out_shape=[
            shape((len(CROSSING), size_y, length), f32),
            shape((5, plan.rows, length), f32),
            shape((DIRECTIONS, size_x, length), f32),
        ],
        in_specs=[VMEM] * (outer + 4),
        out_specs=[VMEM] * 3,
        compiler_params=params(vmem_limit_bytes=6 << 20),
        name="cross",
    )(populations, sites, kept, *came, low, high)
    crossed = lax.ppermute(crossing, "brick", swap)
    partial = pl.pallas_call(
        functools.partial(collide_kernel, plan),
        out_shape=shape(populations.shape, f32),
        in_specs=[VMEM] * 3,
        out_specs=VMEM,
        compiler_params=params(vmem_limit_bytes=6 << 20),
        name="collide",
    )(populations, state, edges)
    read = pl.pallas_call(
        functools.partial(merge_kernel, plan),
        out_shape=shape(populations.shape, f32),
        in_specs=[VMEM, ANY],
        out_specs=ANY,
        scratch_shapes=[pltpu.SemaphoreType.DMA((len(CROSSING),))],
        input_output_aliases={1: 0},
        compiler_params=params(vmem_limit_bytes=4 << 20),
        name="merge",
    )(crossed, partial)
    here = lax.axis_index("brick")
    stay = stay.reshape(1, -1)
    arrived = arrived.reshape(1, -1)
    arrivals = jnp.where(
        here == 0,
        jnp.concatenate([stay, arrived], axis=0),
        jnp.concatenate([arrived, stay], axis=0),
    )
    return (read, moved[None, None], arrivals[None, None])


def solution(mesh):
    placed = (
        P(None, "brick", "chain", None),
        P("brick", "chain", None, None, None),
        P("brick", "chain", None, None),
        P("brick", "chain", None, None),
        P("brick", "chain", None, None),
        P("brick", "chain", None),
        P("brick", "chain", None, None),
        P("brick", "chain", None),
    )

    return jax.shard_map(
        local,
        mesh=mesh,
        in_specs=placed,
        out_specs=(
            P(None, "brick", "chain", None),
            P("brick", "chain", None, None, None),
            P("brick", "chain", None, None),
        ),
        check_vma=False,
    )
```
